512 devices in a mesh: ep: 64 (over x_lo, z, core), blk: 8 (over x_hi, y).
Axes of the slice: x: 4 (x_hi: 2, x_lo: 2; x = x_hi * 2 + x_lo), y: 4, z: 16, core: 2. Of those that a mesh axis runs over, the one named last changes fastest.
Arguments:
- tokens: bfloat16 [4096, 2048], P(('ep', 'blk')), may hold values from -6 to 6
- routes: int32 [4096, 8], P('ep'), may hold values from 0 to 63, all different within a row; in each aligned block of 64 rows (0 to 63, 64 to 127, ...) at most 16 rows name the same one
- gate_scale: bfloat16 [4096, 8], P('ep'), may hold values from 0.099609375 to 1
- placement: int32 [64], replicated, may hold values from 0 to 63, each once
- w_gate: bfloat16 [64, 2048, 1024], P('ep', None, 'blk'), may hold values from -0.125 to 0.125
- w_up: bfloat16 [64, 2048, 1024], P('ep', None, 'blk'), may hold values from -0.125 to 0.125
- w_down: bfloat16 [64, 1024, 2048], P('ep', 'blk'), may hold values from -0.1875 to 0.1875
Outputs:
- mixed: bfloat16 [4096, 2048], P(('ep', 'blk'))
The draws below stay inside these ranges and needn't reach their ends.
Inputs may be any that keep to these rules, and one draw needn't show every extreme that they name: `routes`: in each aligned block of 64 rows (the tokens of one index of ep) no expert is named by more than 16 rows, a bound that some block reaches; a row names 8 different experts. `placement`: each ep index holds exactly one expert.
All inputs are finite; a program needn't handle non-finite values.
Results may differ from the reference program's by a relative error of at most 0.019.
Values may be sent and summed in bfloat16 or wider, within the bound.
A program may use at most 64 MiB of HBM per device.

```python
import math
import jax
import jax.numpy as jnp
import numpy as np
from jax import lax

D = 2048
FF = 1024
TOP = 8
EXPERTS = 64
BLOCK = 64
CAP = 16
FF_PART = 128
TOKENS = 4096
N_EP = 64
N_BLK = 8


def levels(own_key, extent, split, smallest, largest):
    gain, own = 1.0, jax.random.fold_in(own_key, 6)
    for dim, blocks in split:
        steps = jnp.exp(jax.random.uniform(jax.random.fold_in(own, dim), (blocks,), jnp.float32, smallest / len(split), largest / len(split)))
        gain = gain * jnp.repeat(steps, extent[dim] // blocks).reshape([-1 if axis == dim else 1 for axis in range(len(extent))])
    return gain


def routed_block(key, own, number, rows, amount, top, bound, lean):
    sequence = jax.random.permutation(key, amount)
    heavy_load, usual = portions_of(amount, rows * top, bound, lean, True), portions_of(amount, rows * top, bound, lean, False)
    places = jnp.arange(amount)

    def named(sizes, rotation):
        used = int((sizes > 0).sum())
        fixed = max(1, used // 4)
        shifted = fixed + (places - fixed + rotation * (used - fixed)) % max(1, amount - fixed)
        return jnp.zeros((amount,), jnp.int32).at[sequence[jnp.where(places < fixed, places, shifted)]].set(jnp.asarray(sizes, jnp.int32))

    sizes = jnp.where(number % 4 == 0, named(heavy_load, number // 4), named(usual, number - number // 4 - 1))
    mixed = jax.random.permutation(jax.random.fold_in(own, 3), amount)
    source_of, taker = mixed[0:amount // 2 * 2:2], mixed[1:amount // 2 * 2:2]
    margin = jnp.minimum(sizes[source_of] - 1, bound - sizes[taker]) // 2
    margin = jnp.where((source_of == sequence[0]) | (taker == sequence[0]) | (sizes[taker] == 0), 0, jnp.maximum(margin, 0))
    shifted = jax.random.randint(jax.random.fold_in(own, 4), (amount // 2,), 0, 1 << 20) % (margin + 1)
    sizes = sizes.at[source_of].add(-shifted).at[taker].add(shifted)
    members = jnp.searchsorted(jnp.cumsum(sizes), jnp.arange(rows * top), side="right").astype(jnp.int32)
    grid = members.reshape(top, rows).T
    grid = grid[jax.random.permutation(jax.random.fold_in(own, 1), rows)]
    rotation = jax.random.randint(jax.random.fold_in(own, 2), (rows, 1), 0, top)
    return jnp.take_along_axis(grid, (jnp.arange(top)[None, :] + rotation) % top, axis=1)


def portions_of(number_of, total, most, slope, full):
    portions = [(1 << 20) // math.isqrt(grade ** slope) + 1 for grade in range(1, number_of + 1)]
    largest = most if full else min(most, max(-(-total // number_of), total * portions[0] // sum(portions)))
    least = 1 if total - largest >= number_of - 1 else 0
    given, rest = [largest] + [least] * (number_of - 1), total - largest - least * (number_of - 1)
    while rest > 0:
        free = [i for i in range(1, number_of) if given[i] < largest] or [i for i in range(1, number_of) if given[i] < most]
        mass, budget = sum([portions[i] for i in free]), rest
        for i in free:
            addition = min(most - given[i], max(1, budget * portions[i] // mass), rest)
            given[i] = given[i] + addition
            rest = rest - addition
    return np.array(given)


def normal_values(key, shape, scale, bound, cuts=(), kind=jnp.bfloat16):
    factor_of = levels(key, shape, cuts, -0.22, 0.18) if cuts else 1.0
    drawn = jax.random.normal(key, shape, jnp.float32) * scale * factor_of
    return jnp.minimum(jnp.maximum(drawn, -bound), bound).astype(kind)


def setup_inputs(seed: int = 0) -> dict:
    key_of = jax.random.split(jax.random.key(seed), 8)
    tokens = normal_values(key_of[0], (TOKENS, D), 1.0, 6.0, ((0, 512),))
    routes_keys = jax.random.split(jax.random.fold_in(key_of[1], 1), TOKENS // BLOCK)
    routes_turns = jax.random.permutation(jax.random.fold_in(key_of[1], 3), TOKENS // BLOCK)
    routes = jax.vmap(lambda own, number: routed_block(jax.random.fold_in(key_of[1], 2), own, number, BLOCK, EXPERTS, TOP, CAP, 2))(routes_keys, routes_turns).reshape((TOKENS, TOP))
    gate_scale = jnp.clip(jnp.exp(math.log(1.0) - 2.306499 * jax.random.uniform(key_of[2], (TOKENS, TOP), jnp.float32) ** levels(key_of[2], (TOKENS, TOP), ((0, 64),), -0.2, 0.2)), 0.099609375, 1.0).astype(jnp.bfloat16)
    placement = jax.random.permutation(key_of[3], EXPERTS).astype(jnp.int32)
    w_gate = normal_values(key_of[4], (EXPERTS, D, FF), D ** -0.5, 0.125, ((0, 64), (2, 8)))
    w_up = normal_values(key_of[5], (EXPERTS, D, FF), D ** -0.5, 0.125, ((0, 64), (2, 8)))
    w_down = normal_values(key_of[6], (EXPERTS, FF, D), FF ** -0.5, 0.1875, ((0, 64), (1, 8)))
    return dict(tokens=tokens, routes=routes, gate_scale=gate_scale, placement=placement, w_gate=w_gate, w_up=w_up, w_down=w_down)


def reference(tokens, routes, gate_scale, placement, w_gate, w_up, w_down):
    holder = placement[routes]
    row_limit = CAP * N_EP
    scale_full = gate_scale.astype(jnp.float32)

    def add_holder(running, holder_id):
        hit_mask = holder == holder_id
        weight = jnp.sum(jnp.where(hit_mask, scale_full, jnp.float32(0.0)), axis=1)
        chosen = jnp.any(hit_mask, axis=1)
        taken_count = jnp.sum(chosen.astype(jnp.int32))
        token_index = jnp.nonzero(chosen, size=row_limit, fill_value=0)[0].astype(jnp.int32)
        valid_rows = jnp.arange(row_limit, dtype=jnp.int32) < taken_count
        picked = tokens[token_index]
        gate_matrix = lax.dynamic_index_in_dim(w_gate, holder_id, 0, keepdims=False)
        up_matrix = lax.dynamic_index_in_dim(w_up, holder_id, 0, keepdims=False)
        down_matrix = lax.dynamic_index_in_dim(w_down, holder_id, 0, keepdims=False)
        gate_proj = jnp.dot(picked, gate_matrix, preferred_element_type=jnp.float32)
        up_proj = jnp.dot(picked, up_matrix, preferred_element_type=jnp.float32)
        hidden = (jax.nn.silu(gate_proj) * up_proj).astype(jnp.bfloat16)
        partials = jnp.einsum("rjf,jfd->rjd",
                              hidden.reshape(row_limit, N_BLK, FF_PART).astype(jnp.float32),
                              down_matrix.reshape(N_BLK, FF_PART, D).astype(jnp.float32)).astype(jnp.bfloat16)
        row_weight = jnp.where(valid_rows, weight[token_index], jnp.float32(0.0))
        contrib = jnp.sum(partials.astype(jnp.float32), axis=1) * row_weight[:, None]
        return running.at[token_index].add(contrib), None

    start = jnp.zeros((TOKENS, D), jnp.float32)
    running, _ = lax.scan(add_holder, start, jnp.arange(N_EP, dtype=jnp.int32))
    return running.astype(jnp.bfloat16)
```

```python
import jax
import jax.numpy as jnp
from jax import lax
from jax.sharding import Mesh, PartitionSpec as P

AXES = ("xl", "z", "core", "xh", "y")
EP = ("xl", "z", "core")
BLK = ("xh", "y")
PLANE = ("y", "xh", "xl", "z")


def local(tokens, routes, gate_scale, placement, w_gate, w_up, w_down):
    own = tokens.shape[0]
    experts = placement.shape[0]
    blk_index = lax.axis_index("xh") * lax.axis_size("y") + lax.axis_index("y")
    my_routes = lax.dynamic_slice_in_dim(routes, blk_index * own, own, 0)
    my_scale = lax.dynamic_slice_in_dim(gate_scale, blk_index * own, own, 0)
    ids = lax.iota(jnp.int32, experts)
    chosen = my_routes[:, :, None] == ids[None, None, :]
    holder = jnp.sum(jnp.where(chosen, placement[None, None, :], 0), axis=-1)
    dense = jnp.sum(
        jnp.where(holder[:, :, None] == ids[None, None, :], my_scale[:, :, None].astype(jnp.float32), 0.0), axis=1
    ).astype(jnp.bfloat16)
    packed = jnp.concatenate([tokens, dense, jnp.zeros_like(dense)], axis=1)
    everyone = lax.all_gather(packed, "z", axis=0, tiled=True)
    everyone = lax.all_gather(everyone, ("xh", "xl"), axis=0, tiled=True)
    everyone = lax.all_gather(everyone, "y", axis=0, tiled=True)
    width = tokens.shape[1]
    x = everyone[:, :width]
    weights = everyone[:, width : width + experts]
    swap = [(0, 1), (1, 0)]
    wg = jnp.concatenate([w_gate[0], lax.ppermute(w_gate[0], "core", swap)], axis=1)
    wu = jnp.concatenate([w_up[0], lax.ppermute(w_up[0], "core", swap)], axis=1)
    wd = jnp.concatenate([w_down[0], lax.ppermute(w_down[0], "core", swap)], axis=0)
    core = lax.axis_index("core")
    pair = (lax.axis_index("xl") * lax.axis_size("z") + lax.axis_index("z")) * 2
    mine = lax.dynamic_slice_in_dim(weights, pair + core, 1, 1).astype(jnp.float32)
    other = lax.dynamic_slice_in_dim(weights, pair + 1 - core, 1, 1).astype(jnp.float32)
    half = w_down.shape[1]
    first = lax.broadcasted_iota(jnp.int32, (1, 2 * half), 1) < half
    scale = jnp.where(first, mine, other)
    gate = jnp.dot(x, wg, preferred_element_type=jnp.float32)
    up = jnp.dot(x, wu, preferred_element_type=jnp.float32)
    hidden = (jax.nn.silu(gate) * up * scale).astype(jnp.bfloat16)
    out = jnp.dot(hidden, wd, preferred_element_type=jnp.float32).astype(jnp.bfloat16)
    part = lax.psum_scatter(out, "y", scatter_dimension=0, tiled=True)
    part = lax.optimization_barrier(lax.psum_scatter(part, ("xh", "xl"), scatter_dimension=0, tiled=True).astype(jnp.float32))
    total = lax.psum_scatter(part, "z", scatter_dimension=0, tiled=True)
    return lax.optimization_barrier(total).astype(jnp.bfloat16)


def solution(mesh):
    fine = Mesh(mesh.devices.reshape(2, 16, 2, 2, 4), AXES)
    in_specs = (
        P(AXES, None),
        P(EP, None),
        P(EP, None),
        P(),
        P(EP, None, BLK),
        P(EP, None, BLK),
        P(EP, BLK, None),
    )
    return jax.shard_map(local, mesh=fine, in_specs=in_specs, out_specs=P(AXES, None), check_vma=False)
```

```python
import jax
import jax.numpy as jnp
from jax import lax
from jax.sharding import Mesh, PartitionSpec as P

AXES = ("xl", "z", "core", "xh", "y")
EP = ("xl", "z", "core")
BLK = ("xh", "y")


X = ("xl", "xh")
PLACE = {X: (0, 2, 1, 3), "y": (0, 1, 2, 3)}


def step(v, axis, by):
    place = PLACE[axis]
    return lax.ppermute(v, axis, [(place[i], place[(i + by) % 4]) for i in range(4)])


def ring_gather(v, axis):
    half = v.shape[0] // 2
    left = step(v, axis, 1)
    right = step(v, axis, -1)
    return jnp.concatenate([v, left, right, step(left[:half], axis, 1), step(right[half:], axis, -1)], axis=0)


def add(a, b):
    return (a.astype(jnp.float32) + b.astype(jnp.float32)).astype(jnp.bfloat16)


def ring_scatter(v, axis):
    rows = v.shape[0] // 4
    half = rows // 2
    own, left, right, far = (v[k * rows : (k + 1) * rows] for k in range(4))
    from_left = step(far[:half], axis, 1)
    from_right = step(far[half:], axis, -1)
    below = step(right[half:], axis, 1)
    above = step(left[:half], axis, -1)
    first = step(add(right[:half], from_left), axis, 1)
    second = step(add(left[half:], from_right), axis, -1)
    one = jnp.concatenate([first, below], axis=0).astype(jnp.float32)
    two = jnp.concatenate([above, second], axis=0).astype(jnp.float32)
    return own.astype(jnp.float32) + one + two


def swapped(v):
    return v.reshape(4, 4, v.shape[0] // 16, v.shape[1]).transpose(1, 0, 2, 3).reshape(v.shape)


def local(tokens, routes, gate_scale, placement, w_gate, w_up, w_down):
    own = tokens.shape[0]
    experts = placement.shape[0]
    blk_index = lax.axis_index("xh") * lax.axis_size("y") + lax.axis_index("y")
    my_routes = lax.dynamic_slice_in_dim(routes, blk_index * own, own, 0)
    my_scale = lax.dynamic_slice_in_dim(gate_scale, blk_index * own, own, 0)
    ids = lax.iota(jnp.int32, experts)
    chosen = my_routes[:, :, None] == ids[None, None, :]
    holder = jnp.sum(jnp.where(chosen, placement[None, None, :], 0), axis=-1)
    dense = jnp.sum(
        jnp.where(holder[:, :, None] == ids[None, None, :], my_scale[:, :, None].astype(jnp.float32), 0.0), axis=1
    ).astype(jnp.bfloat16)
    packed = jnp.concatenate([dense, jnp.zeros_like(dense), tokens], axis=1)
    everyone = lax.all_gather(packed, "z", axis=0, tiled=True)
    width = tokens.shape[1]
    pad = 2 * experts
    cut = pad + width // 2
    part_a = ring_gather(ring_gather(everyone[:, :cut], X), "y")
    part_b = swapped(ring_gather(ring_gather(everyone[:, cut:], "y"), X))
    x = jnp.concatenate([part_a[:, pad:], part_b], axis=1)
    weights = part_a[:, :experts]
    swap = [(0, 1), (1, 0)]
    wg = jnp.concatenate([w_gate[0], lax.ppermute(w_gate[0], "core", swap)], axis=1)
    wu = jnp.concatenate([w_up[0], lax.ppermute(w_up[0], "core", swap)], axis=1)
    wd = jnp.concatenate([w_down[0], lax.ppermute(w_down[0], "core", swap)], axis=0)
    core = lax.axis_index("core")
    pair = (lax.axis_index("xl") * lax.axis_size("z") + lax.axis_index("z")) * 2
    mine = lax.dynamic_slice_in_dim(weights, pair + core, 1, 1).astype(jnp.float32)
    other = lax.dynamic_slice_in_dim(weights, pair + 1 - core, 1, 1).astype(jnp.float32)
    half = w_down.shape[1]
    first = lax.broadcasted_iota(jnp.int32, (1, 2 * half), 1) < half
    scale = jnp.where(first, mine, other)
    gate = jnp.dot(x, wg, preferred_element_type=jnp.float32)
    up = jnp.dot(x, wu, preferred_element_type=jnp.float32)
    hidden = (jax.nn.silu(gate) * up * scale).astype(jnp.bfloat16)
    out = jnp.dot(hidden, wd, preferred_element_type=jnp.float32).astype(jnp.bfloat16)
    out_a, out_b = out[:, : width // 2], swapped(out[:, width // 2 :])
    sum_a = ring_scatter(ring_scatter(out_a, "y").astype(jnp.bfloat16), X)
    sum_b = ring_scatter(ring_scatter(out_b, X).astype(jnp.bfloat16), "y")
    part = lax.optimization_barrier(jnp.concatenate([sum_a, sum_b], axis=1))
    total = lax.psum_scatter(part, "z", scatter_dimension=0, tiled=True)
    return lax.optimization_barrier(total).astype(jnp.bfloat16)


def solution(mesh):
    fine = Mesh(mesh.devices.reshape(2, 16, 2, 2, 4), AXES)
    in_specs = (
        P(AXES, None),
        P(EP, None),
        P(EP, None),
        P(),
        P(EP, None, BLK),
        P(EP, None, BLK),
        P(EP, BLK, None),
    )
    return jax.shard_map(local, mesh=fine, in_specs=in_specs, out_specs=P(AXES, None), check_vma=False)
```

```python
import jax
import jax.numpy as jnp
from jax import lax
from jax.sharding import Mesh, PartitionSpec as P

AXES = ("xl", "z", "core", "xh", "y")
EP = ("xl", "z", "core")
BLK = ("xh", "y")


X = ("xl", "xh")
PLACE = {X: (0, 2, 1, 3), "y": (0, 1, 2, 3)}


def step(v, axis, by):
    place = PLACE[axis]
    return lax.ppermute(v, axis, [(place[i], place[(i + by) % 4]) for i in range(4)])


def ring_gather(v, axis):
    half = v.shape[0] // 2
    left = step(v, axis, 1)
    right = step(v, axis, -1)
    return jnp.concatenate([v, left, right, step(left[:half], axis, 1), step(right[half:], axis, -1)], axis=0)


def add(a, b):
    return (a.astype(jnp.float32) + b.astype(jnp.float32)).astype(jnp.bfloat16)


def ring_scatter(v, axis):
    rows = v.shape[0] // 4
    half = rows // 2
    own, left, right, far = (v[k * rows : (k + 1) * rows] for k in range(4))
    from_left = step(far[:half], axis, 1)
    from_right = step(far[half:], axis, -1)
    below = step(right[half:], axis, 1)
    above = step(left[:half], axis, -1)
    first = step(add(right[:half], from_left), axis, 1)
    second = step(add(left[half:], from_right), axis, -1)
    one = jnp.concatenate([first, below], axis=0).astype(jnp.float32)
    two = jnp.concatenate([above, second], axis=0).astype(jnp.float32)
    return own.astype(jnp.float32) + one + two


def swapped(v):
    return v.reshape(4, 4, v.shape[0] // 16, v.shape[1]).transpose(1, 0, 2, 3).reshape(v.shape)


def local(tokens, routes, gate_scale, placement, w_gate, w_up, w_down):
    own = tokens.shape[0]
    experts = placement.shape[0]
    blk_index = lax.axis_index("xh") * lax.axis_size("y") + lax.axis_index("y")
    my_routes = lax.dynamic_slice_in_dim(routes, blk_index * own, own, 0)
    my_scale = lax.dynamic_slice_in_dim(gate_scale, blk_index * own, own, 0)
    ids = lax.iota(jnp.int32, experts)
    chosen = my_routes[:, :, None] == ids[None, None, :]
    holder = jnp.sum(jnp.where(chosen, placement[None, None, :], 0), axis=-1)
    dense = jnp.sum(
        jnp.where(holder[:, :, None] == ids[None, None, :], my_scale[:, :, None].astype(jnp.float32), 0.0), axis=1
    ).astype(jnp.bfloat16)
    packed = jnp.concatenate([dense, jnp.zeros_like(dense), tokens], axis=1)
    everyone = lax.all_gather(packed, "z", axis=0, tiled=True)
    width = tokens.shape[1]
    pad = 2 * experts
    cut = pad + width // 2
    part_a = ring_gather(ring_gather(everyone[:, :cut], X), "y")
    part_b = swapped(ring_gather(ring_gather(everyone[:, cut:], "y"), X))
    x = jnp.concatenate([part_a[:, pad:], part_b], axis=1)
    weights = part_a[:, :experts]
    swap = [(0, 1), (1, 0)]
    wg = jnp.concatenate([w_gate[0], lax.ppermute(w_gate[0], "core", swap)], axis=1)
    wu = jnp.concatenate([w_up[0], lax.ppermute(w_up[0], "core", swap)], axis=1)
    wd = jnp.concatenate([w_down[0], lax.ppermute(w_down[0], "core", swap)], axis=0)
    core = lax.axis_index("core")
    pair = (lax.axis_index("xl") * lax.axis_size("z") + lax.axis_index("z")) * 2
    mine = lax.dynamic_slice_in_dim(weights, pair + core, 1, 1).astype(jnp.float32)
    other = lax.dynamic_slice_in_dim(weights, pair + 1 - core, 1, 1).astype(jnp.float32)
    half = w_down.shape[1]
    first = lax.broadcasted_iota(jnp.int32, (1, 2 * half), 1) < half
    scale = jnp.where(first, mine, other)
    gate = jnp.dot(x, wg, preferred_element_type=jnp.float32)
    up = jnp.dot(x, wu, preferred_element_type=jnp.float32)
    hidden = (jax.nn.silu(gate) * up * scale).astype(jnp.bfloat16)
    out = jnp.dot(hidden, wd, preferred_element_type=jnp.float32).astype(jnp.bfloat16)
    out_a, out_b = out[:, : width // 2], swapped(out[:, width // 2 :])
    sum_a = ring_scatter(ring_scatter(out_a, "y").astype(jnp.bfloat16), X)
    sum_b = ring_scatter(ring_scatter(out_b, X).astype(jnp.bfloat16), "y")
    part = lax.optimization_barrier(jnp.concatenate([sum_a, sum_b], axis=1))
    n = lax.axis_size("z")
    block = part.shape[0] // n
    spread = lax.all_to_all(part.astype(jnp.bfloat16), "z", split_axis=0, concat_axis=0, tiled=True)
    return jnp.sum(spread.reshape(n, block, width).astype(jnp.float32), axis=0).astype(jnp.bfloat16)


def solution(mesh):
    fine = Mesh(mesh.devices.reshape(2, 16, 2, 2, 4), AXES)
    in_specs = (
        P(AXES, None),
        P(EP, None),
        P(EP, None),
        P(),
        P(EP, None, BLK),
        P(EP, None, BLK),
        P(EP, BLK, None),
    )
    return jax.shard_map(local, mesh=fine, in_specs=in_specs, out_specs=P(AXES, None), check_vma=False)
```
